128 devices in a mesh: rows: 8 (over z_hi, y), cols: 16 (over z_lo, x, core).
Axes of the slice: x: 4, y: 4, z: 4 (z_hi: 2, z_lo: 2; z = z_hi * 2 + z_lo), core: 2. Of those that a mesh axis runs over, the one named last changes fastest.
Arguments:
- dosage: int32 [512, 24576], P('cols', 'rows'), may hold values from 0 to 2
- present: int32 [512, 24576], P('cols', 'rows'), may hold values from 0 to 1, as said below
- components: float32 [32, 24576], P(None, 'rows'), may hold values from -8 to 8
Outputs:
- kinship: float32 [24576, 24576], P('rows', 'cols')
The draws below stay inside these ranges and needn't reach their ends.
Inputs may be any that keep to these rules, and one draw needn't show every extreme that they name: `present`: markers whose index is a multiple of 8 are observed for every person.
All inputs are finite; a program needn't handle non-finite values.
Results may differ from the reference program's by a relative error of at most 0.0036.
Values may be sent and summed in bfloat16 or wider, within the bound.
A program may use at most 128 MiB of HBM per device.

```python
import jax
import jax.numpy as jnp
from jax import lax

MARKERS = 512
COMPS = 32
PEOPLE_DEV = 3072
PEOPLE = 24576


def ancestry_groups(key):
    return jax.random.randint(jax.random.fold_in(key, 101), (PEOPLE,), 0, 4)


def draw_dosage(key, part):
    groups = ancestry_groups(key)
    percent = jax.random.randint(jax.random.fold_in(key, 102), (MARKERS, 4), 1, 100)
    level = percent[:, groups]
    first = jax.random.randint(jax.random.fold_in(key, 103), (MARKERS, PEOPLE), 0, 100)
    second = jax.random.randint(jax.random.fold_in(key, 104), (MARKERS, PEOPLE), 0, 100)
    return ((first < level).astype(jnp.int32) + (second < level).astype(jnp.int32)).astype(jnp.int32)


def draw_present(key, part):
    roll = jax.random.randint(jax.random.fold_in(key, 201), (MARKERS, PEOPLE), 0, 10)
    marker_index = jnp.arange(MARKERS, dtype=jnp.int32)[:, None]
    always = (marker_index % 8 == 0).astype(jnp.int32)
    return jnp.maximum((roll >= 1).astype(jnp.int32), always).astype(jnp.int32)


def draw_components(key, part):
    groups = ancestry_groups(key)
    centers = 1.5 * jax.random.normal(jax.random.fold_in(key, 105), (COMPS, 4), jnp.float32)
    noise = jax.random.normal(jax.random.fold_in(key, 106), (COMPS, PEOPLE), jnp.float32)
    return jnp.clip(centers[:, groups] + noise, -8.0, 8.0).astype(jnp.float32)


def setup_inputs(seed: int = 0) -> dict:
    key_of = jax.random.split(jax.random.key(seed), 4)
    return {
        "dosage": draw_dosage(jax.random.fold_in(key_of[3], 71), 0),
        "present": draw_present(jax.random.fold_in(key_of[3], 71), 0),
        "components": draw_components(jax.random.fold_in(key_of[3], 71), 0),
    }


def solve_normal(gram, moment):
    width = gram.shape[0]
    index_col = jnp.arange(width, dtype=jnp.int32)[:, None]
    columns = []
    for j in range(width):
        column = gram[:, j, :]
        if j > 0:
            stacked = jnp.stack(columns, axis=1)
            column = column - lax.optimization_barrier(jnp.sum(stacked * stacked[j][None, :, :], axis=1))
        pivot = jnp.sqrt(column[j])
        columns.append(jnp.where(index_col >= j, column / pivot[None, :], jnp.zeros_like(column)))
    factor = jnp.stack(columns, axis=1)
    forward = []
    for j in range(width):
        value = moment[j]
        for k in range(j):
            value = value - factor[j, k] * forward[k]
        forward.append(value / factor[j, j])
    backward = [None] * width
    for j in range(width - 1, -1, -1):
        value = forward[j]
        for k in range(j + 1, width):
            value = value - factor[k, j] * backward[k]
        backward[j] = value / factor[j, j]
    return jnp.stack(backward, axis=0)

def fit_panel(dosage, present, components):
    design = jnp.concatenate([jnp.ones((1, components.shape[1]), jnp.float32), components.astype(jnp.float32)], axis=0)
    width = design.shape[0]
    observed = present.astype(jnp.float32)
    target = 0.5 * dosage.astype(jnp.float32) * observed
    outer_rows = (design[:, None, :] * design[None, :, :]).reshape(width * width, design.shape[1])
    gram_flat = jnp.dot(outer_rows, observed.T, precision=lax.Precision.HIGHEST, preferred_element_type=jnp.float32)
    moment = jnp.dot(design, target.T, precision=lax.Precision.HIGHEST, preferred_element_type=jnp.float32)
    markers_here = observed.shape[0]
    gram = gram_flat.reshape(width, width, markers_here)
    coef = solve_normal(gram, moment)
    fitted = jnp.dot(coef.T, design, precision=lax.Precision.HIGHEST, preferred_element_type=jnp.float32)
    freq = jnp.clip(fitted, 0.01, 0.99)
    resid = (observed * (dosage.astype(jnp.float32) - 2.0 * freq)).astype(jnp.bfloat16)
    sdev = (observed * jnp.sqrt(freq * (1.0 - freq))).astype(jnp.bfloat16)
    return (resid, sdev)

def reference(dosage, present, components):
    resid, sdev = fit_panel(dosage, present, components)
    contract = (((0,), (0,)), ((), ()))
    block = PEOPLE_DEV
    count = PEOPLE // block

    def one_block(index):
        start = (index * block).astype(jnp.int32)
        left_r = lax.dynamic_slice_in_dim(resid, start, block, 1)
        left_s = lax.dynamic_slice_in_dim(sdev, start, block, 1)
        numer = lax.dot_general(left_r, resid, contract, preferred_element_type=jnp.float32)
        denom = lax.dot_general(left_s, sdev, contract, preferred_element_type=jnp.float32)
        return numer / (4.0 * denom)
    tiles = lax.map(one_block, jnp.arange(count, dtype=jnp.int32))
    return tiles.reshape(PEOPLE, PEOPLE)
```

```python
import functools

import jax
import jax.numpy as jnp
from jax import lax
from jax.experimental import pallas as pl
from jax.experimental.pallas import tpu as pltpu
from jax.sharding import PartitionSpec as P

F32 = jnp.float32
BF16 = jnp.bfloat16
MESH = pl.DeviceIdType.MESH

COMPS = 32
WIDTH = 40
CHUNK = 512
OFF = []
for _i in range(COMPS + 1):
    OFF.append(sum(8 * (k // 8 + 1) for k in range(_i)))
GRAM_ROWS = 768
SUMS = 896


def rows_of(i):
    return 8 * (i // 8 + 1)


def split3(value):
    hi = value.astype(BF16).astype(F32)
    rest = value - hi
    mid = rest.astype(BF16).astype(F32)
    low = (rest - mid).astype(BF16).astype(F32)
    return hi, mid, low


def gram_sums(design, own, outer, acc):
    people = design.shape[1]
    acc[...] = jnp.zeros_like(acc)
    outer[OFF[COMPS] + WIDTH:, :] = jnp.zeros((GRAM_ROWS - OFF[COMPS] - WIDTH, CHUNK), F32)

    def chunk(step, carry):
        at = pl.ds(pl.multiple_of(step * CHUNK, CHUNK), CHUNK)
        for i in range(COMPS + 1):
            n = rows_of(i)
            outer[OFF[i]:OFF[i] + n, :] = design[0:n, at] * design[i:i + 1, at]
        left = own[:, :, at].reshape(64, CHUNK)
        value = outer[...]
        total = acc[...]
        for _ in range(3):
            piece = value.astype(BF16)
            total += lax.dot_general(
                left, piece, (((1,), (1,)), ((), ())), preferred_element_type=F32
            )
            value = value - piece.astype(F32)
        acc[...] = total
        return carry

    lax.fori_loop(0, people // CHUNK, chunk, 0)


def solve(gt, bt, inv_s, y_s, xs):
    for j in range(COMPS, -1, -1):
        n = rows_of(j)
        base = OFF[j]
        pivot = gt[pl.ds(base + j, 8, stride=0), :]
        inv = lax.rsqrt(pivot)
        inv = inv * (1.5 - 0.5 * pivot * inv * inv)
        inv_s[j] = inv
        column = [gt[base + 8 * q:base + 8 * q + 8, :] * inv for q in range(n // 8)]
        for q in range(n // 8):
            gt[base + 8 * q:base + 8 * q + 8, :] = column[q]
        y = bt[pl.ds(j, 8, stride=0), :] * inv
        y_s[j] = y
        for q in range(n // 8):
            bt[8 * q:8 * q + 8, :] = bt[8 * q:8 * q + 8, :] - y * column[q]
        for i in range(j - 1, -1, -1):
            factor = gt[pl.ds(base + i, 8, stride=0), :]
            for q in range(i // 8 + 1):
                lo = OFF[i] + 8 * q
                gt[lo:lo + 8, :] = gt[lo:lo + 8, :] - factor * column[q]
    sub = lax.broadcasted_iota(jnp.int32, (8, 128), 0)
    x = [jnp.zeros((8, 128), F32) for _ in range(WIDTH // 8)]
    for j in range(COMPS + 1):
        value = y_s[j]
        if j > 0:
            total = gt[OFF[j]:OFF[j] + 8, :] * x[0]
            for q in range(1, rows_of(j) // 8):
                total += gt[OFF[j] + 8 * q:OFF[j] + 8 * q + 8, :] * x[q]
            value = value - jnp.sum(total, axis=0, keepdims=True)
        value = value * inv_s[j]
        x[j // 8] = jnp.where(sub == j % 8, value, x[j // 8])
    twice = jnp.concatenate(x, axis=0) * 2.0
    hi, mid, low = split3(twice)
    for t, part in enumerate((hi, hi, hi, mid, mid, low)):
        xs[WIDTH * t:WIDTH * t + WIDTH, :] = part
    xs[6 * WIDTH:, :] = jnp.zeros((256 - 6 * WIDTH, 128), F32)


def gather_kernel(dosage, present, comps, a_out, b_out, cb_out, coef_out,
                  own, design, outer, acc, send, recv, wide, gt, bt, inv_s, y_s, xs, coef,
                  ssem, rsem, lsem):
    r = lax.axis_index("rows")
    c = lax.axis_index("cols")
    zh, y = r // 4, r % 4
    zl, x, k = c // 8, (c // 2) % 4, c % 2
    people = dosage.shape[1]
    half = people // 2

    def col(zl_, x_, k_):
        return zl_ * 8 + x_ * 2 + k_

    def row(zh_, y_):
        return zh_ * 4 + y_

    xr, xl, xo = (x + 1) % 4, (x + 3) % 4, (x + 2) % 4
    yr, yl, yo = (y + 1) % 4, (y + 3) % 4, (y + 2) % 4
    zlo, zho, ko = 1 - zl, 1 - zh, 1 - k
    t_row, t_chip = row(zl, x), col(zh, y, 0)
    away = jnp.logical_or(x != y, zh != zl)

    barrier = pltpu.get_barrier_semaphore()
    for d in range(1, 8):
        pl.semaphore_signal(barrier, inc=1, device_id=((r + d) % 8, c), device_id_type=MESH)
    for d in range(1, 16):
        pl.semaphore_signal(barrier, inc=1, device_id=(r, (c + d) % 16), device_id_type=MESH)

    @pl.when(away)
    def _():
        for q in range(2):
            pl.semaphore_signal(barrier, inc=1, device_id=(t_row, t_chip + q), device_id_type=MESH)

    seen = present[...].astype(F32)
    own[0] = (dosage[...].astype(F32) * seen).astype(BF16)
    own[1] = seen.astype(BF16)
    design[0:COMPS, :] = comps[...]
    sub = lax.broadcasted_iota(jnp.int32, (8, people), 0)
    design[COMPS:WIDTH, :] = jnp.where(sub == 0, 1.0, 0.0).astype(F32)

    pl.semaphore_wait(barrier, jnp.where(away, 24, 22))

    sent = []

    def copy(src, dst, idx, dev):
        return pltpu.make_async_remote_copy(
            src_ref=src, dst_ref=dst, send_sem=ssem.at[idx], recv_sem=rsem.at[idx],
            device_id=dev, device_id_type=MESH,
        )

    def push(src, dst, idx, dev):
        one = copy(src, dst, idx, dev)
        one.start()
        sent.append(one)

    def arrive(ref, idx):
        copy(ref, ref, idx, (r, c ^ 1)).wait_recv()

    core_dev = (r, col(zl, x, ko))
    xr_dev, xl_dev = (r, col(zl, xr, k)), (r, col(zl, xl, k))
    zl_dev = (r, col(zlo, x, k))
    yr_dev, yl_dev = (row(zh, yr), c), (row(zh, yl), c)
    zh_dev = (row(zho, y), c)

    mine_t = own.at[:, :, pl.ds(pl.multiple_of(k * half, 128), half)]
    other_t = own.at[:, :, pl.ds(pl.multiple_of(ko * half, 128), half)]
    comps_t = comps.at[:, pl.ds(pl.multiple_of(k * half, 128), half)]
    other_dev = (t_row, t_chip + ko)
    t0 = copy(mine_t, b_out.at[c], 20, (t_row, t_chip + k))
    t2 = copy(comps_t, cb_out, 22, (t_row, t_chip + k))
    here0 = pltpu.make_async_copy(mine_t, b_out.at[c], lsem.at[1])
    here2 = pltpu.make_async_copy(comps_t, cb_out, lsem.at[2])

    @pl.when(away)
    def _():
        t0.start()

    @pl.when(jnp.logical_not(away))
    def _():
        here0.start()

    push(other_t, b_out.at[c], 21, other_dev)

    @pl.when(away)
    def _():
        t2.start()

    @pl.when(jnp.logical_not(away))
    def _():
        here2.start()

    keep = pltpu.make_async_copy(own, a_out.at[c], lsem.at[0])
    keep.start()
    push(own, a_out.at[c], 1, zl_dev)
    push(own, a_out.at[c], 2, xr_dev)
    push(own, a_out.at[c], 3, xl_dev)
    push(own, a_out.at[c], 0, core_dev)

    gram_sums(design, own, outer, acc)
    for q in range(4):
        send[q, :, 0:GRAM_ROWS] = acc[32 + 8 * q:40 + 8 * q, :]
        send[q, :, GRAM_ROWS:SUMS] = 0.5 * acc[8 * q:8 * q + 8, OFF[COMPS]:OFF[COMPS] + 128]
    wide[...] = jnp.zeros_like(wide)
    for d in range(1, 8):
        to = (r + d) % 8
        push(send.at[to % 4], recv.at[d], 31 + d, (to, c))

    t_slot = row(zh, y)

    def pair(zh_, y_):
        return b_out.at[pl.ds(2 * row(zh_, y_), 2)]

    def single(zh_, y_, h):
        return b_out.at[2 * row(zh_, y_) + h]

    @pl.when(away)
    def _():
        copy(mine_t, single(zh, y, k), 20, (t_row, t_chip + k)).wait_recv()
        copy(comps_t, cb_out, 22, (t_row, t_chip + k)).wait_recv()

    @pl.when(jnp.logical_not(away))
    def _():
        here0.wait()
        here2.wait()

    copy(other_t, single(zh, y, ko), 21, other_dev).wait_recv()
    push(pair(zh, y), pair(zh, y), 23, zh_dev)
    push(pair(zh, y), pair(zh, y), 24, yr_dev)
    push(pair(zh, y), pair(zh, y), 25, yl_dev)

    total = send[r % 4]
    for d in range(1, 8):
        arrive(recv.at[d], 31 + d)
        total = total + recv[d]
    wide[0:8, :] = total
    for q in range(SUMS // 128):
        block = wide[:, 128 * q:128 * q + 128].T
        if q < GRAM_ROWS // 128:
            gt[128 * q:128 * q + 128, :] = block
        else:
            bt[...] = block[0:WIDTH]
    solve(gt, bt, inv_s, y_s, xs)
    for q in range(2):
        coef[:, 128 * q:128 * q + 128] = xs[128 * q:128 * q + 128, :].T[0:8]
    keep_coef = pltpu.make_async_copy(coef, coef_out.at[c, y], lsem.at[3])
    keep_coef.start()
    for d in range(1, 4):
        push(coef, coef_out.at[c, y], 38 + d, (row(zh, (y + d) % 4), c))

    def slot(zl_, x_, k_):
        return a_out.at[col(zl_, x_, k_)]

    def slot_half(zl_, x_, k_, h):
        return a_out.at[col(zl_, x_, k_), h]

    arrive(slot(zlo, x, k), 1)
    push(slot(zlo, x, k), slot(zlo, x, k), 4, xr_dev)
    push(slot(zlo, x, k), slot(zlo, x, k), 5, xl_dev)
    push(slot(zlo, x, k), slot(zlo, x, k), 6, core_dev)
    arrive(slot(zl, xl, k), 2)
    push(slot_half(zl, xl, k, 0), slot_half(zl, xl, k, 0), 7, xr_dev)
    push(slot(zl, xl, k), slot(zl, xl, k), 9, core_dev)
    arrive(slot(zl, xr, k), 3)
    push(slot_half(zl, xr, k, 1), slot_half(zl, xr, k, 1), 8, xl_dev)
    push(slot(zl, xr, k), slot(zl, xr, k), 10, core_dev)

    arrive(pair(zho, y), 23)
    push(pair(zho, y), pair(zho, y), 26, yr_dev)
    push(pair(zho, y), pair(zho, y), 27, yl_dev)
    arrive(pair(zh, yl), 24)
    push(single(zh, yl, 0), single(zh, yl, 0), 28, yr_dev)
    arrive(pair(zh, yr), 25)
    push(single(zh, yr, 1), single(zh, yr, 1), 29, yl_dev)

    for d in range(1, 4):
        arrive(coef_out.at[c, (y + 4 - d) % 4], 38 + d)
    keep_coef.wait()
    for d in range(1, 16):
        push(coef_out.at[c], coef_out.at[c], 41 + d, (r, (c + d) % 16))

    arrive(slot(zlo, xl, k), 4)
    push(slot_half(zlo, xl, k, 0), slot_half(zlo, xl, k, 0), 11, xr_dev)
    push(slot(zlo, xl, k), slot(zlo, xl, k), 13, core_dev)
    arrive(slot(zlo, xr, k), 5)
    push(slot_half(zlo, xr, k, 1), slot_half(zlo, xr, k, 1), 12, xl_dev)
    push(slot(zlo, xr, k), slot(zlo, xr, k), 14, core_dev)
    arrive(pair(zho, yl), 26)
    push(single(zho, yl, 0), single(zho, yl, 0), 30, yr_dev)
    arrive(pair(zho, yr), 27)
    push(single(zho, yr, 1), single(zho, yr, 1), 31, yl_dev)

    arrive(slot_half(zl, xo, k, 0), 7)
    arrive(slot_half(zl, xo, k, 1), 8)
    push(slot(zl, xo, k), slot(zl, xo, k), 15, core_dev)
    arrive(slot_half(zlo, xo, k, 0), 11)
    arrive(slot_half(zlo, xo, k, 1), 12)
    push(slot(zlo, xo, k), slot(zlo, xo, k), 16, core_dev)

    arrive(single(zh, yo, 0), 28)
    arrive(single(zh, yo, 1), 29)
    arrive(single(zho, yo, 0), 30)
    arrive(single(zho, yo, 1), 31)
    arrive(slot(zl, x, ko), 0)
    arrive(slot(zlo, x, ko), 6)
    arrive(slot(zl, xl, ko), 9)
    arrive(slot(zl, xr, ko), 10)
    arrive(slot(zlo, xl, ko), 13)
    arrive(slot(zlo, xr, ko), 14)
    arrive(slot(zl, xo, ko), 15)
    arrive(slot(zlo, xo, ko), 16)
    for d in range(1, 16):
        arrive(coef_out.at[(c + 16 - d) % 16], 41 + d)

    keep.wait()

    @pl.when(away)
    def _():
        t0.wait_send()
        t2.wait_send()

    for one in sent:
        one.wait_send()


def gather(dosage, present, comps):
    markers, people = dosage.shape
    half = people // 2
    any_space = pl.BlockSpec(memory_space=pl.ANY)
    vmem = pl.BlockSpec(memory_space=pltpu.VMEM)
    return pl.pallas_call(
        gather_kernel,
        out_shape=(
            jax.ShapeDtypeStruct((16, 2, markers, people), BF16),
            jax.ShapeDtypeStruct((16, 2, markers, half), BF16),
            jax.ShapeDtypeStruct((COMPS, half), F32),
            jax.ShapeDtypeStruct((16, 4, 8, 256), F32),
        ),
        in_specs=[vmem] * 3,
        out_specs=(any_space,) * 4,
        scratch_shapes=[
            pltpu.VMEM((2, markers, people), BF16),
            pltpu.VMEM((WIDTH, people), F32),
            pltpu.VMEM((GRAM_ROWS, CHUNK), F32),
            pltpu.VMEM((64, GRAM_ROWS), F32),
            pltpu.VMEM((4, 8, SUMS), F32),
            pltpu.VMEM((8, 8, SUMS), F32),
            pltpu.VMEM((128, SUMS), F32),
            pltpu.VMEM((GRAM_ROWS, 128), F32),
            pltpu.VMEM((WIDTH, 128), F32),
            pltpu.VMEM((COMPS + 1, 8, 128), F32),
            pltpu.VMEM((COMPS + 1, 8, 128), F32),
            pltpu.VMEM((256, 128), F32),
            pltpu.VMEM((8, 256), F32),
            pltpu.SemaphoreType.DMA((60,)),
            pltpu.SemaphoreType.DMA((60,)),
            pltpu.SemaphoreType.DMA((4,)),
        ],
        compiler_params=pltpu.CompilerParams(collective_id=0, has_side_effects=True),
        name="gather_fit",
    )(dosage, present, comps)


def form(raw, comps, coef, stack, resid, sdev):
    width = comps.shape[1]
    hi, mid, low = split3(comps)
    sub = lax.broadcasted_iota(jnp.int32, (8, width), 0)
    ones = jnp.where(sub == 0, 1.0, 0.0).astype(F32)
    zeros = jnp.zeros((8, width), F32)
    for t, part in enumerate((hi, mid, low, hi, mid, hi)):
        stack[WIDTH * t:WIDTH * t + COMPS, :] = part
        stack[WIDTH * t + COMPS:WIDTH * (t + 1), :] = ones if part is hi else zeros
    stack[6 * WIDTH:, :] = jnp.zeros((256 - 6 * WIDTH, width), F32)
    twice = jnp.dot(coef, stack[...].astype(BF16), preferred_element_type=F32)
    twice = jnp.clip(twice, 0.02, 1.98)
    counts = raw[:, 0].reshape(512, width)
    seen = raw[:, 1].reshape(512, width)
    resid[...] = (counts.astype(F32) - twice).astype(BF16) * seen
    spread = twice * (2.0 - twice)
    sdev[...] = (spread * lax.rsqrt(spread)).astype(BF16) * seen


def ratio_kernel(a_ref, b_ref, ca_ref, cb_ref, coef_ref, out_ref,
                 rb, sb, ra, sa, stack_a, stack_b):
    coef = coef_ref[...].astype(BF16)

    @pl.when(pl.program_id(0) == 0)
    def _():
        for h in range(3):
            at = slice(512 * h, 512 * h + 512)
            form(b_ref[:, :, :, at], cb_ref[:, at], coef, stack_b, rb.at[:, at], sb.at[:, at])

    form(a_ref[...], ca_ref[...], coef, stack_a, ra, sa)
    contract = (((0,), (0,)), ((), ()))
    numer = lax.dot_general(ra[...], rb[...], contract, preferred_element_type=F32)
    denom = lax.dot_general(sa[...], sb[...], contract, preferred_element_type=F32)
    out_ref[...] = numer / denom


def ratio(a_raw, b_raw, comps, comps_b, coef):
    people = comps.shape[1]
    half = people // 2
    tile = 256
    whole = lambda shape: pl.BlockSpec(shape, lambda i: (0,) * len(shape), pipeline_mode=pl.Buffered(1))
    return pl.pallas_call(
        ratio_kernel,
        out_shape=jax.ShapeDtypeStruct((people, half), F32),
        grid=(people // tile,),
        in_specs=[
            pl.BlockSpec((16, 2, 32, tile), lambda i: (0, 0, 0, i)),
            whole((16, 2, 32, half)),
            pl.BlockSpec((COMPS, tile), lambda i: (0, i)),
            whole((COMPS, half)),
            whole((512, 256)),
        ],
        out_specs=pl.BlockSpec((tile, half), lambda i: (i, 0)),
        scratch_shapes=[
            pltpu.VMEM((512, half), BF16),
            pltpu.VMEM((512, half), BF16),
            pltpu.VMEM((512, tile), BF16),
            pltpu.VMEM((512, tile), BF16),
            pltpu.VMEM((256, tile), F32),
            pltpu.VMEM((256, 512), F32),
        ],
        name="form_ratio",
    )(a_raw, b_raw, comps, comps_b, coef)


def per_device(dosage, present, comps):
    a_raw, b_raw, comps_b, coef = gather(dosage, present, comps)
    return ratio(a_raw, b_raw, comps, comps_b, coef.reshape(512, 256))


def solution(mesh):
    placed = (P("cols", "rows"), P("cols", "rows"), P(None, "rows"))
    return jax.shard_map(
        per_device, mesh=mesh, in_specs=placed, out_specs=P("rows", "cols"), check_vma=False
    )
```

```python
import functools

import jax
import jax.numpy as jnp
from jax import lax
from jax.experimental import pallas as pl
from jax.experimental.pallas import tpu as pltpu
from jax.sharding import PartitionSpec as P

F32 = jnp.float32
BF16 = jnp.bfloat16
MESH = pl.DeviceIdType.MESH

COMPS = 32
WIDTH = 40
CHUNK = 512
OFF = []
for _i in range(COMPS + 1):
    OFF.append(sum(8 * (k // 8 + 1) for k in range(_i)))
GRAM_ROWS = 768
SUMS = 896


def rows_of(i):
    return 8 * (i // 8 + 1)


def split3(value):
    hi = value.astype(BF16).astype(F32)
    rest = value - hi
    mid = rest.astype(BF16).astype(F32)
    low = (rest - mid).astype(BF16).astype(F32)
    return hi, mid, low


def gram_sums(design, own, outer, acc):
    people = design.shape[1]
    acc[...] = jnp.zeros_like(acc)
    outer[OFF[COMPS] + WIDTH:, :] = jnp.zeros((GRAM_ROWS - OFF[COMPS] - WIDTH, CHUNK), F32)

    def chunk(step, carry):
        at = pl.ds(pl.multiple_of(step * CHUNK, CHUNK), CHUNK)
        for i in range(COMPS + 1):
            n = rows_of(i)
            outer[OFF[i]:OFF[i] + n, :] = design[0:n, at] * design[i:i + 1, at]
        left = own[:, :, at].reshape(64, CHUNK)
        value = outer[...]
        total = acc[...]
        for _ in range(3):
            piece = value.astype(BF16)
            total += lax.dot_general(
                left, piece, (((1,), (1,)), ((), ())), preferred_element_type=F32
            )
            value = value - piece.astype(F32)
        acc[...] = total
        return carry

    lax.fori_loop(0, people // CHUNK, chunk, 0)


def solve(gt, bt, inv_s, y_s, xs):
    for j in range(COMPS, -1, -1):
        n = rows_of(j)
        base = OFF[j]
        pivot = gt[pl.ds(base + j, 8, stride=0), :]
        inv = lax.rsqrt(pivot)
        inv = inv * (1.5 - 0.5 * pivot * inv * inv)
        inv_s[j] = inv
        column = [gt[base + 8 * q:base + 8 * q + 8, :] * inv for q in range(n // 8)]
        for q in range(n // 8):
            gt[base + 8 * q:base + 8 * q + 8, :] = column[q]
        y = bt[pl.ds(j, 8, stride=0), :] * inv
        y_s[j] = y
        for q in range(n // 8):
            bt[8 * q:8 * q + 8, :] = bt[8 * q:8 * q + 8, :] - y * column[q]
        for i in range(j - 1, -1, -1):
            factor = gt[pl.ds(base + i, 8, stride=0), :]
            for q in range(i // 8 + 1):
                lo = OFF[i] + 8 * q
                gt[lo:lo + 8, :] = gt[lo:lo + 8, :] - factor * column[q]
    sub = lax.broadcasted_iota(jnp.int32, (8, 128), 0)
    x = [jnp.zeros((8, 128), F32) for _ in range(WIDTH // 8)]
    for j in range(COMPS + 1):
        value = y_s[j]
        if j > 0:
            total = gt[OFF[j]:OFF[j] + 8, :] * x[0]
            for q in range(1, rows_of(j) // 8):
                total += gt[OFF[j] + 8 * q:OFF[j] + 8 * q + 8, :] * x[q]
            value = value - jnp.sum(total, axis=0, keepdims=True)
        value = value * inv_s[j]
        x[j // 8] = jnp.where(sub == j % 8, value, x[j // 8])
    twice = jnp.concatenate(x, axis=0) * 2.0
    for t, part in enumerate(split3(twice)):
        xs[WIDTH * t:WIDTH * t + WIDTH, :] = part
    xs[3 * WIDTH:, :] = jnp.zeros((128 - 3 * WIDTH, 128), F32)


def gather_kernel(dosage, present, comps, a_out, b_out, cb_out, coef_out,
                  own, relay, relay_z, relay_c, design, outer, acc, send, recv, wide, gt, bt,
                  inv_s, y_s, xs, coef, ssem, rsem, lsem):
    r = lax.axis_index("rows")
    c = lax.axis_index("cols")
    zh, y = r // 4, r % 4
    zl, x, k = c // 8, (c // 2) % 4, c % 2
    people = dosage.shape[1]
    half = people // 2

    def col(zl_, x_, k_):
        return zl_ * 8 + x_ * 2 + k_

    def row(zh_, y_):
        return zh_ * 4 + y_

    xr, xl, xo = (x + 1) % 4, (x + 3) % 4, (x + 2) % 4
    yr, yl, yo = (y + 1) % 4, (y + 3) % 4, (y + 2) % 4
    zlo, zho, ko = 1 - zl, 1 - zh, 1 - k
    turn = [[(x - y + 4 + 2 * p + q) % 4 for q in range(2)] for p in range(2)]
    turn_mine = [(x - y + 4 + 2 * p + k) % 4 for p in range(2)]
    turn_other = [(x - y + 4 + 2 * p + ko) % 4 for p in range(2)]
    swapped = zh != zl

    barrier = pltpu.get_barrier_semaphore()
    for d in range(1, 8):
        pl.semaphore_signal(barrier, inc=1, device_id=((r + d) % 8, c), device_id_type=MESH)
    for d in range(1, 16):
        pl.semaphore_signal(barrier, inc=1, device_id=(r, (c + d) % 16), device_id_type=MESH)

    pl.semaphore_signal(
        barrier, inc=1, device_id=(row(zho, y), col(zlo, x, k)), device_id_type=MESH
    )

    @pl.when(swapped)
    def _():
        for q in range(8):
            pl.semaphore_signal(
                barrier, inc=1, device_id=(row(zl, y), zh * 8 + q), device_id_type=MESH
            )

    seen = present[...].astype(F32)
    own[0] = (dosage[...].astype(F32) * seen).astype(BF16)
    own[1] = seen.astype(BF16)
    design[0:COMPS, :] = comps[...]
    sub = lax.broadcasted_iota(jnp.int32, (8, people), 0)
    design[COMPS:WIDTH, :] = jnp.where(sub == 0, 1.0, 0.0).astype(F32)

    pl.semaphore_wait(barrier, jnp.where(swapped, 31, 23))

    sent = []
    names = {}

    def copy(src, dst, name, dev):
        idx = names.setdefault(name, len(names))
        return pltpu.make_async_remote_copy(
            src_ref=src, dst_ref=dst, send_sem=ssem.at[idx], recv_sem=rsem.at[idx],
            device_id=dev, device_id_type=MESH,
        )

    def push(src, dst, name, dev):
        one = copy(src, dst, name, dev)
        one.start()
        sent.append(one.wait_send)

    def pass_on(ref, name, dev):
        push(ref, ref, name, dev)

    core_dev = (r, col(zl, x, ko))

    def arrive(ref, name):
        copy(ref, ref, name, core_dev).wait_recv()

    def push_or_keep(here, src, dst, name, dev):
        one = copy(src, dst, name, dev)
        local = pltpu.make_async_copy(src, dst, lsem.at[names[name]])

        @pl.when(here)
        def _():
            local.start()

        @pl.when(jnp.logical_not(here))
        def _():
            one.start()

        def finish():
            @pl.when(jnp.logical_not(here))
            def _():
                one.wait_send()

        sent.append(finish)

    def arrive_or_keep(here, ref, name):
        one = copy(ref, ref, name, core_dev)
        local = pltpu.make_async_copy(ref, ref, lsem.at[names[name]])

        @pl.when(here)
        def _():
            local.wait()

        @pl.when(jnp.logical_not(here))
        def _():
            one.wait_recv()

    xr_dev, xl_dev = (r, col(zl, xr, k)), (r, col(zl, xl, k))
    zl_dev = (r, col(zlo, x, k))
    yr_dev, yl_dev = (row(zh, yr), c), (row(zh, yl), c)
    crosses = [zl == 1, zl == 0]
    z_dev = [(row(jnp.where(crosses[p], zho, zh), y), col(zlo, x, k)) for p in range(2)]
    zh_from = [jnp.where(crosses[1 - p], zho, zh) for p in range(2)]

    def a_slot(zl_, x_, k_, p=None):
        ref = a_out.at[col(zl_, x_, k_)]
        return ref if p is None else ref.at[p]

    def piece(ref, at):
        return ref.at[pl.ds(pl.multiple_of(8 * at, 8), 8)]

    def people_half(ref, q):
        return ref.at[:, pl.ds(pl.multiple_of(q * half, 128), half)]

    def leg1(p, q):
        push_or_keep(turn[p][q] == y, people_half(own.at[p], q), relay.at[p, q],
                     f"leg1_{p}{q}", (row(zh, turn[p][q]), c))

    leg1(0, 0)
    leg1(0, 1)
    push(own.at[0], a_slot(zl, x, k, 0), "own_xr0", xr_dev)
    push(own.at[0], a_slot(zl, x, k, 0), "own_xl0", xl_dev)
    push(own.at[0], a_slot(zl, x, k, 0), "own_zl0", zl_dev)
    leg1(1, 0)
    leg1(1, 1)
    push_or_keep(turn_mine[0] == y, people_half(piece(comps, turn_mine[0]), k), relay_c,
                 "leg1_c", (row(zh, turn_mine[0]), c))
    push(own.at[1], a_slot(zl, x, k, 1), "own_zl1", zl_dev)
    push(own, a_slot(zl, x, k), "own_core", core_dev)
    keep = pltpu.make_async_copy(own, a_out.at[c], lsem.at[127])
    keep.start()

    gram_sums(design, own, outer, acc)
    for q in range(4):
        send[q, :, 0:GRAM_ROWS] = acc[32 + 8 * q:40 + 8 * q, :]
        send[q, :, GRAM_ROWS:SUMS] = 0.5 * acc[8 * q:8 * q + 8, OFF[COMPS]:OFF[COMPS] + 128]
    wide[...] = jnp.zeros_like(wide)
    for d in range(1, 8):
        to = (r + d) % 8
        push(send.at[to % 4], recv.at[d], ("rs", d), (to, c))

    def home(p):
        return jnp.logical_and(zh == zl, turn_mine[p] == x)

    def leg2(p):
        chip_row = row(zl, y)
        for q in range(2):
            arrive_or_keep(turn[p][q] == y, relay.at[p, q], f"leg1_{p}{q}")
        push_or_keep(home(p), relay.at[p, k], b_out.at[p, c],
                     f"leg2_{p}_same", (chip_row, col(zh, turn_mine[p], k)))
        push(relay.at[p, ko], b_out.at[p, c],
             f"leg2_{p}_other", (chip_row, col(zh, turn_other[p], ko)))

    def leg2_c():
        arrive_or_keep(turn_mine[0] == y, relay_c, "leg1_c")
        push_or_keep(home(0), relay_c, piece(cb_out, y),
                     "leg2_c_same", (row(zl, y), col(zh, turn_mine[0], k)))

    def b_one(p, zh_, y_, k_):
        return b_out.at[p, 2 * row(zh_, (x + y_ + 8 - 2 * p - k) % 4) + k_]

    leg2(0)
    leg2(1)
    push(own.at[1], a_slot(zl, x, k, 1), "own_xr1", xr_dev)
    push(own.at[1], a_slot(zl, x, k, 1), "own_xl1", xl_dev)
    leg2_c()

    for p in range(2):
        arrive(a_slot(zlo, x, k, p), f"own_zl{p}")
        pass_on(a_slot(zlo, x, k, p), f"zl_xr{p}", xr_dev)
        pass_on(a_slot(zlo, x, k, p), f"zl_xl{p}", xl_dev)
    pass_on(a_slot(zlo, x, k), "zl_core", core_dev)

    core_of = [k, ko]

    def start_column(p, e):
        ref = b_one(p, zh, y, core_of[e])
        if e == 0:
            arrive_or_keep(home(p), ref, f"leg2_{p}_same")
        else:
            arrive(ref, f"leg2_{p}_other")
        push(ref, relay_z.at[p, e], f"b_mid{p}{e}", z_dev[p])
        pass_on(ref, f"b_yr{p}{e}", yr_dev)
        pass_on(ref, f"b_yl{p}{e}", yl_dev)

    def relay_column(p, e):
        arrive(relay_z.at[p, e], f"b_mid{p}{e}")
        push(relay_z.at[p, e], b_one(p, zh_from[p], y, core_of[e]), f"b_zh{p}{e}", z_dev[p])

    def turn_column(p, e):
        ref = b_one(p, zho, y, core_of[e])
        arrive(ref, f"b_zh{p}{e}")
        pass_on(ref, f"bz_yr{p}{e}", yr_dev)
        pass_on(ref, f"bz_yl{p}{e}", yl_dev)

    def far_column(p, e, zh_, tag):
        right, left = b_one(p, zh_, yl, core_of[e]), b_one(p, zh_, yr, core_of[e])
        arrive(right, f"{tag}_yr{p}{e}")
        arrive(left, f"{tag}_yl{p}{e}")
        if p == 0:
            pass_on(right, f"{tag}_far{p}{e}", yr_dev)
        else:
            pass_on(left, f"{tag}_far{p}{e}", yl_dev)

    parts = [(p, e) for p in range(2) for e in range(2)]
    for p, e in parts:
        start_column(p, e)
    for p, e in parts:
        relay_column(p, e)
    arrive_or_keep(home(0), piece(cb_out, y), "leg2_c_same")
    pass_on(piece(cb_out, y), "c_yr", yr_dev)
    pass_on(piece(cb_out, y), "c_yl", yl_dev)

    total = send[r % 4]
    for d in range(1, 8):
        arrive(recv.at[d], ("rs", d))
        total = total + recv[d]
    wide[0:8, :] = total
    for q in range(SUMS // 128):
        block = wide[:, 128 * q:128 * q + 128].T
        if q < GRAM_ROWS // 128:
            gt[128 * q:128 * q + 128, :] = block
        else:
            bt[...] = block[0:WIDTH]
    solve(gt, bt, inv_s, y_s, xs)
    coef[...] = xs[...].T[0:8]
    keep_coef = pltpu.make_async_copy(coef, coef_out.at[c, y], lsem.at[126])
    keep_coef.start()
    for d in range(1, 4):
        push(coef, coef_out.at[c, y], ("cag", d), (row(zh, (y + d) % 4), c))

    for p in range(2):
        arrive(a_slot(zl, xl, k, p), f"own_xr{p}")
        arrive(a_slot(zl, xr, k, p), f"own_xl{p}")
        if p == 0:
            pass_on(a_slot(zl, xl, k, 0), "far_xr", xr_dev)
        else:
            pass_on(a_slot(zl, xr, k, 1), "far_xl", xl_dev)
    pass_on(a_slot(zl, xl, k), "xl_core", core_dev)
    pass_on(a_slot(zl, xr, k), "xr_core", core_dev)

    for p, e in parts:
        far_column(p, e, zh, "b")
    for p, e in parts:
        turn_column(p, e)
    arrive(piece(cb_out, yl), "c_yr")
    pass_on(piece(cb_out, yl), "c_far", yr_dev)
    arrive(piece(cb_out, yr), "c_yl")

    for d in range(1, 4):
        arrive(coef_out.at[c, (y + 4 - d) % 4], ("cag", d))
    keep_coef.wait()
    for d in range(1, 16):
        push(coef_out.at[c], coef_out.at[c], ("rag", d), (r, (c + d) % 16))

    for p in range(2):
        arrive(a_slot(zlo, xl, k, p), f"zl_xr{p}")
        arrive(a_slot(zlo, xr, k, p), f"zl_xl{p}")
        if p == 0:
            pass_on(a_slot(zlo, xl, k, 0), "zfar_xr", xr_dev)
        else:
            pass_on(a_slot(zlo, xr, k, 1), "zfar_xl", xl_dev)
    pass_on(a_slot(zlo, xl, k), "zxl_core", core_dev)
    pass_on(a_slot(zlo, xr, k), "zxr_core", core_dev)
    for p, e in parts:
        far_column(p, e, zho, "bz")

    arrive(a_slot(zl, xo, k, 0), "far_xr")
    arrive(a_slot(zl, xo, k, 1), "far_xl")
    pass_on(a_slot(zl, xo, k), "far_core", core_dev)
    for p, e in parts:
        arrive(b_one(p, zh, yo, core_of[e]), f"b_far{p}{e}")
    arrive(piece(cb_out, yo), "c_far")
    arrive(a_slot(zlo, xo, k, 0), "zfar_xr")
    arrive(a_slot(zlo, xo, k, 1), "zfar_xl")
    pass_on(a_slot(zlo, xo, k), "zfar_core", core_dev)
    for p, e in parts:
        arrive(b_one(p, zho, yo, core_of[e]), f"bz_far{p}{e}")

    arrive(a_slot(zl, x, ko), "own_core")
    arrive(a_slot(zlo, x, ko), "zl_core")
    arrive(a_slot(zl, xl, ko), "xl_core")
    arrive(a_slot(zl, xr, ko), "xr_core")
    arrive(a_slot(zlo, xl, ko), "zxl_core")
    arrive(a_slot(zlo, xr, ko), "zxr_core")
    arrive(a_slot(zl, xo, ko), "far_core")
    arrive(a_slot(zlo, xo, ko), "zfar_core")
    for d in range(1, 16):
        arrive(coef_out.at[(c + 16 - d) % 16], ("rag", d))
    keep.wait()
    for finish in sent:
        finish()


def gather(dosage, present, comps):
    markers, people = dosage.shape
    half = people // 2
    any_space = pl.BlockSpec(memory_space=pl.ANY)
    vmem = pl.BlockSpec(memory_space=pltpu.VMEM)
    return pl.pallas_call(
        gather_kernel,
        out_shape=(
            jax.ShapeDtypeStruct((16, 2, markers, people), BF16),
            jax.ShapeDtypeStruct((2, 16, markers, half), BF16),
            jax.ShapeDtypeStruct((COMPS, half), F32),
            jax.ShapeDtypeStruct((16, 4, 8, 128), F32),
        ),
        in_specs=[vmem] * 3,
        out_specs=(any_space,) * 4,
        scratch_shapes=[
            pltpu.VMEM((2, markers, people), BF16),
            pltpu.VMEM((2, 2, markers, half), BF16),
            pltpu.VMEM((2, 2, markers, half), BF16),
            pltpu.VMEM((8, half), F32),
            pltpu.VMEM((WIDTH, people), F32),
            pltpu.VMEM((GRAM_ROWS, CHUNK), F32),
            pltpu.VMEM((64, GRAM_ROWS), F32),
            pltpu.VMEM((4, 8, SUMS), F32),
            pltpu.VMEM((8, 8, SUMS), F32),
            pltpu.VMEM((128, SUMS), F32),
            pltpu.VMEM((GRAM_ROWS, 128), F32),
            pltpu.VMEM((WIDTH, 128), F32),
            pltpu.VMEM((COMPS + 1, 8, 128), F32),
            pltpu.VMEM((COMPS + 1, 8, 128), F32),
            pltpu.VMEM((128, 128), F32),
            pltpu.VMEM((8, 128), F32),
            pltpu.SemaphoreType.DMA((128,)),
            pltpu.SemaphoreType.DMA((128,)),
            pltpu.SemaphoreType.DMA((128,)),
        ],
        compiler_params=pltpu.CompilerParams(collective_id=0, has_side_effects=True),
        name="gather_fit",
    )(dosage, present, comps)


def form(counts, seen, comps, coef, stack, resid, sdev):
    width = comps.shape[1]
    hi, mid, low = split3(comps)
    sub = lax.broadcasted_iota(jnp.int32, (8, width), 0)
    ones = jnp.where(sub == 0, 1.0, 0.0).astype(F32)
    zeros = jnp.zeros((8, width), F32)
    stack[...] = jnp.zeros_like(stack)
    for group, parts in ((0, (hi, hi, hi)), (128, (mid, mid)), (256, (low,))):
        for t, part in enumerate(parts):
            at = group + WIDTH * t
            stack[at:at + COMPS, :] = part
            stack[at + COMPS:at + WIDTH, :] = ones if part is hi else zeros
    right = stack[...].astype(BF16)
    twice = jnp.dot(jnp.concatenate([coef, coef], axis=1), right[0:256], preferred_element_type=F32)
    twice += jnp.dot(coef, right[256:384], preferred_element_type=F32)
    twice = jnp.clip(twice, 0.02, 1.98)
    resid[...] = (counts.astype(F32) - twice).astype(BF16) * seen
    spread = twice * (2.0 - twice)
    sdev[...] = (spread * lax.rsqrt(spread)).astype(BF16) * seen


def ratio_kernel(a_ref, b_ref, ca_ref, cb_ref, coef_ref, out_ref,
                 rb, sb, ra, sa, stack_a, stack_b):
    coef = coef_ref[...].astype(BF16)

    @pl.when(pl.program_id(0) == 0)
    def _():
        for h in range(3):
            at = slice(512 * h, 512 * h + 512)
            form(b_ref[0, :, :, at].reshape(512, 512), b_ref[1, :, :, at].reshape(512, 512),
                 cb_ref[:, at], coef, stack_b, rb.at[:, at], sb.at[:, at])

    tile = ra.shape[1]
    form(a_ref[:, 0].reshape(512, tile), a_ref[:, 1].reshape(512, tile),
         ca_ref[...], coef, stack_a, ra, sa)
    contract = (((0,), (0,)), ((), ()))
    numer = lax.dot_general(ra[...], rb[...], contract, preferred_element_type=F32)
    denom = lax.dot_general(sa[...], sb[...], contract, preferred_element_type=F32)
    out_ref[...] = numer / denom


def ratio(a_raw, b_raw, comps, comps_b, coef):
    people = comps.shape[1]
    half = people // 2
    tile = 256
    whole = lambda shape: pl.BlockSpec(shape, lambda i: (0,) * len(shape), pipeline_mode=pl.Buffered(1))
    return pl.pallas_call(
        ratio_kernel,
        out_shape=jax.ShapeDtypeStruct((people, half), F32),
        grid=(people // tile,),
        in_specs=[
            pl.BlockSpec((16, 2, 32, tile), lambda i: (0, 0, 0, i)),
            whole((2, 16, 32, half)),
            pl.BlockSpec((COMPS, tile), lambda i: (0, i)),
            whole((COMPS, half)),
            whole((512, 128)),
        ],
        out_specs=pl.BlockSpec((tile, half), lambda i: (i, 0)),
        scratch_shapes=[
            pltpu.VMEM((512, half), BF16),
            pltpu.VMEM((512, half), BF16),
            pltpu.VMEM((512, tile), BF16),
            pltpu.VMEM((512, tile), BF16),
            pltpu.VMEM((384, tile), F32),
            pltpu.VMEM((384, 512), F32),
        ],
        name="form_ratio",
    )(a_raw, b_raw, comps, comps_b, coef)


def per_device(dosage, present, comps):
    a_raw, b_raw, comps_b, coef = gather(dosage, present, comps)
    return ratio(a_raw, b_raw, comps, comps_b, coef.reshape(512, 128))


def solution(mesh):
    placed = (P("cols", "rows"), P("cols", "rows"), P(None, "rows"))
    return jax.shard_map(
        per_device, mesh=mesh, in_specs=placed, out_specs=P("rows", "cols"), check_vma=False
    )
```

```python
import functools

import jax
import jax.numpy as jnp
from jax import lax
from jax.experimental import pallas as pl
from jax.experimental.pallas import tpu as pltpu
from jax.sharding import PartitionSpec as P

F32 = jnp.float32
BF16 = jnp.bfloat16
MESH = pl.DeviceIdType.MESH

COMPS = 32
WIDTH = 40
CHUNK = 512
OFF = []
for _i in range(COMPS + 1):
    OFF.append(sum(8 * (k // 8 + 1) for k in range(_i)))
GRAM_ROWS = 768
SUMS = 896


def rows_of(i):
    return 8 * (i // 8 + 1)


def split3(value):
    hi = value.astype(BF16).astype(F32)
    rest = value - hi
    mid = rest.astype(BF16).astype(F32)
    low = (rest - mid).astype(BF16).astype(F32)
    return hi, mid, low


def gram_sums(design, own, outer, acc):
    people = design.shape[1]
    acc[...] = jnp.zeros_like(acc)
    outer[OFF[COMPS] + WIDTH:, :] = jnp.zeros((GRAM_ROWS - OFF[COMPS] - WIDTH, CHUNK), F32)

    def chunk(step, carry):
        at = pl.ds(pl.multiple_of(step * CHUNK, CHUNK), CHUNK)
        for i in range(COMPS + 1):
            n = rows_of(i)
            outer[OFF[i]:OFF[i] + n, :] = design[0:n, at] * design[i:i + 1, at]
        left = own[:, :, at].reshape(64, CHUNK)
        value = outer[...]
        total = acc[...]
        for _ in range(3):
            piece = value.astype(BF16)
            total += lax.dot_general(
                left, piece, (((1,), (1,)), ((), ())), preferred_element_type=F32
            )
            value = value - piece.astype(F32)
        acc[...] = total
        return carry

    lax.fori_loop(0, people // CHUNK, chunk, 0)


def solve(gt, bt, inv_s, y_s, xs):
    for j in range(COMPS, -1, -1):
        n = rows_of(j)
        base = OFF[j]
        pivot = gt[pl.ds(base + j, 8, stride=0), :]
        inv = lax.rsqrt(pivot)
        inv = inv * (1.5 - 0.5 * pivot * inv * inv)
        inv_s[j] = inv
        column = [gt[base + 8 * q:base + 8 * q + 8, :] * inv for q in range(n // 8)]
        for q in range(n // 8):
            gt[base + 8 * q:base + 8 * q + 8, :] = column[q]
        y = bt[pl.ds(j, 8, stride=0), :] * inv
        y_s[j] = y
        for q in range(n // 8):
            bt[8 * q:8 * q + 8, :] = bt[8 * q:8 * q + 8, :] - y * column[q]
        for i in range(j - 1, -1, -1):
            factor = gt[pl.ds(base + i, 8, stride=0), :]
            for q in range(i // 8 + 1):
                lo = OFF[i] + 8 * q
                gt[lo:lo + 8, :] = gt[lo:lo + 8, :] - factor * column[q]
    sub = lax.broadcasted_iota(jnp.int32, (8, 128), 0)
    x = [jnp.zeros((8, 128), F32) for _ in range(WIDTH // 8)]
    for j in range(COMPS + 1):
        value = y_s[j]
        if j > 0:
            total = gt[OFF[j]:OFF[j] + 8, :] * x[0]
            for q in range(1, rows_of(j) // 8):
                total += gt[OFF[j] + 8 * q:OFF[j] + 8 * q + 8, :] * x[q]
            value = value - jnp.sum(total, axis=0, keepdims=True)
        value = value * inv_s[j]
        x[j // 8] = jnp.where(sub == j % 8, value, x[j // 8])
    twice = jnp.concatenate(x, axis=0) * 2.0
    for t, part in enumerate(split3(twice)):
        xs[WIDTH * t:WIDTH * t + WIDTH, :] = part
    xs[3 * WIDTH:, :] = jnp.zeros((128 - 3 * WIDTH, 128), F32)


def gather_kernel(dosage, present, comps, a_out, b_out, cb_out, coef_out,
                  own, relay, relay_z, relay_c, design, outer, acc, send, recv, wide, gt, bt,
                  inv_s, y_s, xs, coef, ssem, rsem, lsem):
    r = lax.axis_index("rows")
    c = lax.axis_index("cols")
    zh, y = r // 4, r % 4
    zl, x, k = c // 8, (c // 2) % 4, c % 2
    people = dosage.shape[1]
    half = people // 2

    def col(zl_, x_, k_):
        return zl_ * 8 + x_ * 2 + k_

    def row(zh_, y_):
        return zh_ * 4 + y_

    xr, xl, xo = (x + 1) % 4, (x + 3) % 4, (x + 2) % 4
    yr, yl, yo = (y + 1) % 4, (y + 3) % 4, (y + 2) % 4
    zlo, zho, ko = 1 - zl, 1 - zh, 1 - k
    turn = [[(x - y + 4 + 2 * p + q) % 4 for q in range(2)] for p in range(2)]
    turn_mine = [(x - y + 4 + 2 * p + k) % 4 for p in range(2)]
    turn_other = [(x - y + 4 + 2 * p + ko) % 4 for p in range(2)]
    swapped = zh != zl

    barrier = pltpu.get_barrier_semaphore()
    for d in range(1, 8):
        pl.semaphore_signal(barrier, inc=1, device_id=((r + d) % 8, c), device_id_type=MESH)
    for d in range(1, 16):
        pl.semaphore_signal(barrier, inc=1, device_id=(r, (c + d) % 16), device_id_type=MESH)

    pl.semaphore_signal(
        barrier, inc=1, device_id=(row(zho, y), col(zlo, x, k)), device_id_type=MESH
    )

    @pl.when(swapped)
    def _():
        for q in range(8):
            pl.semaphore_signal(
                barrier, inc=1, device_id=(row(zl, y), zh * 8 + q), device_id_type=MESH
            )

    seen = present[...].astype(F32)
    own[0] = (dosage[...].astype(F32) * seen).astype(BF16)
    own[1] = seen.astype(BF16)
    design[0:COMPS, :] = comps[...]
    sub = lax.broadcasted_iota(jnp.int32, (8, people), 0)
    design[COMPS:WIDTH, :] = jnp.where(sub == 0, 1.0, 0.0).astype(F32)

    pl.semaphore_wait(barrier, jnp.where(swapped, 31, 23))

    sent = []
    names = {}

    def copy(src, dst, name, dev):
        idx = names.setdefault(name, len(names))
        return pltpu.make_async_remote_copy(
            src_ref=src, dst_ref=dst, send_sem=ssem.at[idx], recv_sem=rsem.at[idx],
            device_id=dev, device_id_type=MESH,
        )

    def push(src, dst, name, dev):
        one = copy(src, dst, name, dev)
        one.start()
        sent.append(one.wait_send)

    def pass_on(ref, name, dev):
        push(ref, ref, name, dev)

    core_dev = (r, col(zl, x, ko))

    def arrive(ref, name):
        copy(ref, ref, name, core_dev).wait_recv()

    def push_or_keep(here, src, dst, name, dev):
        one = copy(src, dst, name, dev)
        local = pltpu.make_async_copy(src, dst, lsem.at[names[name]])

        @pl.when(here)
        def _():
            local.start()

        @pl.when(jnp.logical_not(here))
        def _():
            one.start()

        def finish():
            @pl.when(jnp.logical_not(here))
            def _():
                one.wait_send()

        sent.append(finish)

    def arrive_or_keep(here, ref, name):
        one = copy(ref, ref, name, core_dev)
        local = pltpu.make_async_copy(ref, ref, lsem.at[names[name]])

        @pl.when(here)
        def _():
            local.wait()

        @pl.when(jnp.logical_not(here))
        def _():
            one.wait_recv()

    xr_dev, xl_dev = (r, col(zl, xr, k)), (r, col(zl, xl, k))
    zl_dev = (r, col(zlo, x, k))
    yr_dev, yl_dev = (row(zh, yr), c), (row(zh, yl), c)
    crosses = [zl == 1, zl == 0]
    z_dev = [(row(jnp.where(crosses[p], zho, zh), y), col(zlo, x, k)) for p in range(2)]
    zh_from = [jnp.where(crosses[1 - p], zho, zh) for p in range(2)]

    def a_slot(zl_, x_, k_, p=None):
        ref = a_out.at[col(zl_, x_, k_)]
        return ref if p is None else ref.at[p]

    def piece(ref, at):
        return ref.at[pl.ds(pl.multiple_of(8 * at, 8), 8)]

    def people_half(ref, q):
        return ref.at[:, pl.ds(pl.multiple_of(q * half, 128), half)]

    def leg1(p, q):
        push_or_keep(turn[p][q] == y, people_half(own.at[p], q), relay.at[p, q],
                     f"leg1_{p}{q}", (row(zh, turn[p][q]), c))

    leg1(0, 0)
    leg1(0, 1)
    push(own.at[0], a_slot(zl, x, k, 0), "own_xr0", xr_dev)
    push(own.at[0], a_slot(zl, x, k, 0), "own_xl0", xl_dev)
    push(own.at[0], a_slot(zl, x, k, 0), "own_zl0", zl_dev)
    leg1(1, 0)
    leg1(1, 1)
    push_or_keep(turn_mine[0] == y, people_half(piece(comps, turn_mine[0]), k), relay_c,
                 "leg1_c", (row(zh, turn_mine[0]), c))
    push(own.at[1], a_slot(zl, x, k, 1), "own_zl1", zl_dev)
    push(own, a_slot(zl, x, k), "own_core", core_dev)
    keep = pltpu.make_async_copy(own, a_out.at[c], lsem.at[127])
    keep.start()

    gram_sums(design, own, outer, acc)
    for q in range(4):
        send[q, :, 0:GRAM_ROWS] = acc[32 + 8 * q:40 + 8 * q, :]
        send[q, :, GRAM_ROWS:SUMS] = 0.5 * acc[8 * q:8 * q + 8, OFF[COMPS]:OFF[COMPS] + 128]
    wide[...] = jnp.zeros_like(wide)
    for d in range(1, 8):
        to = (r + d) % 8
        push(send.at[to % 4], recv.at[d], ("rs", d), (to, c))

    def home(p):
        return jnp.logical_and(zh == zl, turn_mine[p] == x)

    def leg2(p):
        chip_row = row(zl, y)
        for q in range(2):
            arrive_or_keep(turn[p][q] == y, relay.at[p, q], f"leg1_{p}{q}")
        push_or_keep(home(p), relay.at[p, k], b_out.at[p, c],
                     f"leg2_{p}_same", (chip_row, col(zh, turn_mine[p], k)))
        push(relay.at[p, ko], b_out.at[p, c],
             f"leg2_{p}_other", (chip_row, col(zh, turn_other[p], ko)))

    def leg2_c():
        arrive_or_keep(turn_mine[0] == y, relay_c, "leg1_c")
        push_or_keep(home(0), relay_c, piece(cb_out, y),
                     "leg2_c_same", (row(zl, y), col(zh, turn_mine[0], k)))

    def b_one(p, zh_, y_, k_):
        return b_out.at[p, 2 * row(zh_, (x + y_ + 8 - 2 * p - k) % 4) + k_]

    leg2(0)
    leg2(1)
    push(own.at[1], a_slot(zl, x, k, 1), "own_xr1", xr_dev)
    push(own.at[1], a_slot(zl, x, k, 1), "own_xl1", xl_dev)
    leg2_c()

    for p in range(2):
        arrive(a_slot(zlo, x, k, p), f"own_zl{p}")
        pass_on(a_slot(zlo, x, k, p), f"zl_xr{p}", xr_dev)
        pass_on(a_slot(zlo, x, k, p), f"zl_xl{p}", xl_dev)
    pass_on(a_slot(zlo, x, k), "zl_core", core_dev)

    core_of = [k, ko]

    def start_column(p, e):
        ref = b_one(p, zh, y, core_of[e])
        if e == 0:
            arrive_or_keep(home(p), ref, f"leg2_{p}_same")
        else:
            arrive(ref, f"leg2_{p}_other")
        push(ref, relay_z.at[p, e], f"b_mid{p}{e}", z_dev[p])
        pass_on(ref, f"b_yr{p}{e}", yr_dev)
        pass_on(ref, f"b_yl{p}{e}", yl_dev)

    def relay_column(p, e):
        arrive(relay_z.at[p, e], f"b_mid{p}{e}")
        push(relay_z.at[p, e], b_one(p, zh_from[p], y, core_of[e]), f"b_zh{p}{e}", z_dev[p])

    def turn_column(p, e):
        ref = b_one(p, zho, y, core_of[e])
        arrive(ref, f"b_zh{p}{e}")
        pass_on(ref, f"bz_yr{p}{e}", yr_dev)
        pass_on(ref, f"bz_yl{p}{e}", yl_dev)

    def far_column(p, e, zh_, tag):
        right, left = b_one(p, zh_, yl, core_of[e]), b_one(p, zh_, yr, core_of[e])
        arrive(right, f"{tag}_yr{p}{e}")
        arrive(left, f"{tag}_yl{p}{e}")
        if p == 0:
            pass_on(right, f"{tag}_far{p}{e}", yr_dev)
        else:
            pass_on(left, f"{tag}_far{p}{e}", yl_dev)

    parts = [(p, e) for p in range(2) for e in range(2)]
    for p, e in parts:
        start_column(p, e)
    for p, e in parts:
        relay_column(p, e)
    arrive_or_keep(home(0), piece(cb_out, y), "leg2_c_same")
    pass_on(piece(cb_out, y), "c_yr", yr_dev)
    pass_on(piece(cb_out, y), "c_yl", yl_dev)

    total = send[r % 4]
    for d in range(1, 8):
        arrive(recv.at[d], ("rs", d))
        total = total + recv[d]
    wide[0:8, :] = total
    for q in range(SUMS // 128):
        block = wide[:, 128 * q:128 * q + 128].T
        if q < GRAM_ROWS // 128:
            gt[128 * q:128 * q + 128, :] = block
        else:
            bt[...] = block[0:WIDTH]
    solve(gt, bt, inv_s, y_s, xs)
    coef[...] = xs[...].T[0:8]
    keep_coef = pltpu.make_async_copy(coef, coef_out.at[c, y], lsem.at[126])
    keep_coef.start()
    for d in range(1, 4):
        push(coef, coef_out.at[c, y], ("cag", d), (row(zh, (y + d) % 4), c))

    for p in range(2):
        arrive(a_slot(zl, xl, k, p), f"own_xr{p}")
        arrive(a_slot(zl, xr, k, p), f"own_xl{p}")
        if p == 0:
            pass_on(a_slot(zl, xl, k, 0), "far_xr", xr_dev)
        else:
            pass_on(a_slot(zl, xr, k, 1), "far_xl", xl_dev)
    pass_on(a_slot(zl, xl, k), "xl_core", core_dev)
    pass_on(a_slot(zl, xr, k), "xr_core", core_dev)

    for p, e in parts:
        far_column(p, e, zh, "b")
    for p, e in parts:
        turn_column(p, e)
    arrive(piece(cb_out, yl), "c_yr")
    pass_on(piece(cb_out, yl), "c_far", yr_dev)
    arrive(piece(cb_out, yr), "c_yl")

    for d in range(1, 4):
        arrive(coef_out.at[c, (y + 4 - d) % 4], ("cag", d))
    keep_coef.wait()
    for d in range(1, 16):
        push(coef_out.at[c], coef_out.at[c], ("rag", d), (r, (c + d) % 16))

    for p in range(2):
        arrive(a_slot(zlo, xl, k, p), f"zl_xr{p}")
        arrive(a_slot(zlo, xr, k, p), f"zl_xl{p}")
        if p == 0:
            pass_on(a_slot(zlo, xl, k, 0), "zfar_xr", xr_dev)
        else:
            pass_on(a_slot(zlo, xr, k, 1), "zfar_xl", xl_dev)
    pass_on(a_slot(zlo, xl, k), "zxl_core", core_dev)
    pass_on(a_slot(zlo, xr, k), "zxr_core", core_dev)
    for p, e in parts:
        far_column(p, e, zho, "bz")

    arrive(a_slot(zl, xo, k, 0), "far_xr")
    arrive(a_slot(zl, xo, k, 1), "far_xl")
    pass_on(a_slot(zl, xo, k), "far_core", core_dev)
    for p, e in parts:
        arrive(b_one(p, zh, yo, core_of[e]), f"b_far{p}{e}")
    arrive(piece(cb_out, yo), "c_far")
    arrive(a_slot(zlo, xo, k, 0), "zfar_xr")
    arrive(a_slot(zlo, xo, k, 1), "zfar_xl")
    pass_on(a_slot(zlo, xo, k), "zfar_core", core_dev)
    for p, e in parts:
        arrive(b_one(p, zho, yo, core_of[e]), f"bz_far{p}{e}")

    arrive(a_slot(zl, x, ko), "own_core")
    arrive(a_slot(zlo, x, ko), "zl_core")
    arrive(a_slot(zl, xl, ko), "xl_core")
    arrive(a_slot(zl, xr, ko), "xr_core")
    arrive(a_slot(zlo, xl, ko), "zxl_core")
    arrive(a_slot(zlo, xr, ko), "zxr_core")
    arrive(a_slot(zl, xo, ko), "far_core")
    arrive(a_slot(zlo, xo, ko), "zfar_core")
    for d in range(1, 16):
        arrive(coef_out.at[(c + 16 - d) % 16], ("rag", d))
    keep.wait()
    for finish in sent:
        finish()


def gather(dosage, present, comps):
    markers, people = dosage.shape
    half = people // 2
    any_space = pl.BlockSpec(memory_space=pl.ANY)
    vmem = pl.BlockSpec(memory_space=pltpu.VMEM)
    return pl.pallas_call(
        gather_kernel,
        out_shape=(
            jax.ShapeDtypeStruct((16, 2, markers, people), BF16),
            jax.ShapeDtypeStruct((2, 16, markers, half), BF16),
            jax.ShapeDtypeStruct((COMPS, half), F32),
            jax.ShapeDtypeStruct((16, 4, 8, 128), F32),
        ),
        in_specs=[vmem] * 3,
        out_specs=(any_space,) * 4,
        scratch_shapes=[
            pltpu.VMEM((2, markers, people), BF16),
            pltpu.VMEM((2, 2, markers, half), BF16),
            pltpu.VMEM((2, 2, markers, half), BF16),
            pltpu.VMEM((8, half), F32),
            pltpu.VMEM((WIDTH, people), F32),
            pltpu.VMEM((GRAM_ROWS, CHUNK), F32),
            pltpu.VMEM((64, GRAM_ROWS), F32),
            pltpu.VMEM((4, 8, SUMS), F32),
            pltpu.VMEM((8, 8, SUMS), F32),
            pltpu.VMEM((128, SUMS), F32),
            pltpu.VMEM((GRAM_ROWS, 128), F32),
            pltpu.VMEM((WIDTH, 128), F32),
            pltpu.VMEM((COMPS + 1, 8, 128), F32),
            pltpu.VMEM((COMPS + 1, 8, 128), F32),
            pltpu.VMEM((128, 128), F32),
            pltpu.VMEM((8, 128), F32),
            pltpu.SemaphoreType.DMA((128,)),
            pltpu.SemaphoreType.DMA((128,)),
            pltpu.SemaphoreType.DMA((128,)),
        ],
        compiler_params=pltpu.CompilerParams(collective_id=0, has_side_effects=True),
        name="gather_fit",
    )(dosage, present, comps)


def form(counts, seen, comps, coef, stack, resid, sdev):
    width = comps.shape[1]
    hi, mid, low = split3(comps)
    sub = lax.broadcasted_iota(jnp.int32, (8, width), 0)
    ones = jnp.where(sub == 0, 1.0, 0.0).astype(F32)
    zeros = jnp.zeros((8, width), F32)
    for at, part in ((0, hi), (40, hi), (80, hi), (128, mid), (168, mid), (208, low)):
        stack[at:at + COMPS, :] = part
        stack[at + COMPS:at + WIDTH, :] = ones if part is hi else zeros
    for at in (120, 248):
        stack[at:at + 8, :] = zeros
    twice = jnp.dot(coef, stack[...].astype(BF16), preferred_element_type=F32)
    twice = jnp.clip(twice, 0.02, 1.98)
    resid[...] = (counts.astype(F32) - twice).astype(BF16) * seen
    spread = twice * (2.0 - twice)
    sdev[...] = (spread * lax.rsqrt(spread)).astype(BF16) * seen


def ratio_kernel(steps, a0_ref, a1_ref, a2_ref, b_ref, c0_ref, c1_ref, c2_ref, cb_ref, coef_ref, out_ref,
                 left, rb, sb, ra0, sa0, ra1, sa1, stack, stack_b):
    tile = ra0.shape[1]
    half = rb.shape[1]
    piece = 256

    def form_a(a_ref, c_ref, ra, sa, h):
        at = slice(piece * h, piece * h + piece)
        form(a_ref[:, 0, :, at].reshape(512, piece), a_ref[:, 1, :, at].reshape(512, piece),
             c_ref[:, at], left[...], stack.at[h], ra.at[:, at], sa.at[:, at])

    @pl.when(pl.program_id(0) == 0)
    def _():
        base = coef_ref[...]
        lane = lax.broadcasted_iota(jnp.int32, base.shape, 1)
        left[:, 0:128] = base.astype(BF16)
        left[:, 128:256] = jnp.where(lane < 2 * WIDTH, base, pltpu.roll(base, 2 * WIDTH, 1)).astype(BF16)
        for h in range(half // 512):
            at = slice(512 * h, 512 * h + 512)
            form(b_ref[0, :, :, at].reshape(512, 512), b_ref[1, :, :, at].reshape(512, 512),
                 cb_ref[:, at], left[...], stack_b, rb.at[:, at], sb.at[:, at])
        for h in range(tile // piece):
            form_a(a0_ref, c0_ref, ra0, sa0, h)

    contract = (((0,), (0,)), ((), ()))

    def phase(ra, sa, row, a_ref, c_ref, rn, sn):
        for h in range(half // 256):
            at = slice(256 * h, 256 * h + 256)
            numer = lax.dot_general(ra[...], rb[:, at], contract, preferred_element_type=F32)
            denom = lax.dot_general(sa[...], sb[:, at], contract, preferred_element_type=F32)
            out_ref[row:row + tile, at] = numer / denom
            if h < tile // piece:
                form_a(a_ref, c_ref, rn, sn, h)

    phase(ra0, sa0, 0, a1_ref, c1_ref, ra1, sa1)
    phase(ra1, sa1, tile, a2_ref, c2_ref, ra0, sa0)


def ratio(a_raw, b_raw, comps, comps_b, coef):
    people = comps.shape[1]
    half = people // 2
    tile = 256
    tiles = people // tile
    whole = lambda shape: pl.BlockSpec(shape, lambda i: (0,) * len(shape), pipeline_mode=pl.Buffered(1))
    first = lambda i: 0
    odd = lambda i: 2 * i + 1
    even = lambda i: jnp.minimum(2 * i + 2, tiles - 2)
    a_spec = lambda at: pl.BlockSpec((16, 2, 32, tile), lambda i: (0, 0, 0, at(i)))
    c_spec = lambda at: pl.BlockSpec((COMPS, tile), lambda i: (0, at(i)))
    return pl.pallas_call(
        functools.partial(ratio_kernel, tiles // 2),
        out_shape=jax.ShapeDtypeStruct((people, half), F32),
        grid=(tiles // 2,),
        in_specs=[
            pl.BlockSpec((16, 2, 32, tile), lambda i: (0, 0, 0, 0), pipeline_mode=pl.Buffered(1)),
            a_spec(odd), a_spec(even),
            whole((2, 16, 32, half)),
            pl.BlockSpec((COMPS, tile), lambda i: (0, 0), pipeline_mode=pl.Buffered(1)),
            c_spec(odd), c_spec(even),
            whole((COMPS, half)),
            whole((512, 128)),
        ],
        out_specs=pl.BlockSpec((2 * tile, half), lambda i: (i, 0)),
        scratch_shapes=[
            pltpu.VMEM((512, 256), BF16),
            pltpu.VMEM((512, half), BF16),
            pltpu.VMEM((512, half), BF16),
            pltpu.VMEM((512, tile), BF16),
            pltpu.VMEM((512, tile), BF16),
            pltpu.VMEM((512, tile), BF16),
            pltpu.VMEM((512, tile), BF16),
            pltpu.VMEM((tile // 256, 256, 256), F32),
            pltpu.VMEM((256, 512), F32),
        ],
        name="form_ratio",
    )(a_raw, a_raw, a_raw, b_raw, comps, comps, comps, comps_b, coef)


def per_device(dosage, present, comps):
    a_raw, b_raw, comps_b, coef = gather(dosage, present, comps)
    return ratio(a_raw, b_raw, comps, comps_b, coef.reshape(512, 128))


def solution(mesh):
    placed = (P("cols", "rows"), P("cols", "rows"), P(None, "rows"))
    return jax.shard_map(
        per_device, mesh=mesh, in_specs=placed, out_specs=P("rows", "cols"), check_vma=False
    )
```

```python
import functools

import jax
import jax.numpy as jnp
from jax import lax
from jax.experimental import pallas as pl
from jax.experimental.pallas import tpu as pltpu
from jax.sharding import PartitionSpec as P

F32 = jnp.float32
BF16 = jnp.bfloat16
MESH = pl.DeviceIdType.MESH

COMPS = 32
WIDTH = 40
CHUNK = 512
OFF = []
for _i in range(COMPS + 1):
    OFF.append(sum(8 * (k // 8 + 1) for k in range(_i)))
GRAM_ROWS = 768
SUMS = 896


def rows_of(i):
    return 8 * (i // 8 + 1)


def split3(value):
    hi = value.astype(BF16).astype(F32)
    rest = value - hi
    mid = rest.astype(BF16).astype(F32)
    low = (rest - mid).astype(BF16).astype(F32)
    return hi, mid, low


def gram_sums(design, own, outer, acc):
    people = design.shape[1]
    acc[...] = jnp.zeros_like(acc)
    outer[OFF[COMPS] + WIDTH:, :] = jnp.zeros((GRAM_ROWS - OFF[COMPS] - WIDTH, CHUNK), F32)

    def chunk(step, carry):
        at = pl.ds(pl.multiple_of(step * CHUNK, CHUNK), CHUNK)
        for i in range(COMPS + 1):
            n = rows_of(i)
            outer[OFF[i]:OFF[i] + n, :] = design[0:n, at] * design[i:i + 1, at]
        left = own[:, :, at].reshape(64, CHUNK)
        value = outer[...]
        total = acc[...]
        for _ in range(3):
            piece = value.astype(BF16)
            total += lax.dot_general(
                left, piece, (((1,), (1,)), ((), ())), preferred_element_type=F32
            )
            value = value - piece.astype(F32)
        acc[...] = total
        return carry

    lax.fori_loop(0, people // CHUNK, chunk, 0)


def solve(gt, bt, inv_s, y_s, xs):
    for j in range(COMPS, -1, -1):
        n = rows_of(j)
        base = OFF[j]
        pivot = gt[pl.ds(base + j, 8, stride=0), :]
        inv = lax.rsqrt(pivot)
        inv = inv * (1.5 - 0.5 * pivot * inv * inv)
        inv_s[j] = inv
        column = [gt[base + 8 * q:base + 8 * q + 8, :] * inv for q in range(n // 8)]
        for q in range(n // 8):
            gt[base + 8 * q:base + 8 * q + 8, :] = column[q]
        y = bt[pl.ds(j, 8, stride=0), :] * inv
        y_s[j] = y
        for q in range(n // 8):
            bt[8 * q:8 * q + 8, :] = bt[8 * q:8 * q + 8, :] - y * column[q]
        for i in range(j - 1, -1, -1):
            factor = gt[pl.ds(base + i, 8, stride=0), :]
            for q in range(i // 8 + 1):
                lo = OFF[i] + 8 * q
                gt[lo:lo + 8, :] = gt[lo:lo + 8, :] - factor * column[q]
    sub = lax.broadcasted_iota(jnp.int32, (8, 128), 0)
    x = [jnp.zeros((8, 128), F32) for _ in range(WIDTH // 8)]
    for j in range(COMPS + 1):
        value = y_s[j]
        if j > 0:
            total = gt[OFF[j]:OFF[j] + 8, :] * x[0]
            for q in range(1, rows_of(j) // 8):
                total += gt[OFF[j] + 8 * q:OFF[j] + 8 * q + 8, :] * x[q]
            value = value - jnp.sum(total, axis=0, keepdims=True)
        value = value * inv_s[j]
        x[j // 8] = jnp.where(sub == j % 8, value, x[j // 8])
    twice = jnp.concatenate(x, axis=0) * 2.0
    for t, part in enumerate(split3(twice)):
        xs[WIDTH * t:WIDTH * t + WIDTH, :] = part
    xs[3 * WIDTH:, :] = jnp.zeros((128 - 3 * WIDTH, 128), F32)


def gather_kernel(dosage, present, comps, a_out, b_out, cb_out, coef_out,
                  own, relay, relay_z, relay_c, design, outer, acc, send, recv, wide, gt, bt,
                  inv_s, y_s, xs, coef, ssem, rsem, lsem):
    r = lax.axis_index("rows")
    c = lax.axis_index("cols")
    zh, y = r // 4, r % 4
    zl, x, k = c // 8, (c // 2) % 4, c % 2
    people = dosage.shape[1]
    half = people // 2

    def col(zl_, x_, k_):
        return zl_ * 8 + x_ * 2 + k_

    def row(zh_, y_):
        return zh_ * 4 + y_

    xr, xl, xo = (x + 1) % 4, (x + 3) % 4, (x + 2) % 4
    yr, yl, yo = (y + 1) % 4, (y + 3) % 4, (y + 2) % 4
    zlo, zho, ko = 1 - zl, 1 - zh, 1 - k
    turn = [[(x - y + 4 + 2 * p + q) % 4 for q in range(2)] for p in range(2)]
    turn_mine = [(x - y + 4 + 2 * p + k) % 4 for p in range(2)]
    turn_other = [(x - y + 4 + 2 * p + ko) % 4 for p in range(2)]
    swapped = zh != zl

    barrier = pltpu.get_barrier_semaphore()
    for d in range(1, 8):
        pl.semaphore_signal(barrier, inc=1, device_id=((r + d) % 8, c), device_id_type=MESH)
    for d in range(1, 16):
        pl.semaphore_signal(barrier, inc=1, device_id=(r, (c + d) % 16), device_id_type=MESH)

    pl.semaphore_signal(
        barrier, inc=1, device_id=(row(zho, y), col(zlo, x, k)), device_id_type=MESH
    )

    @pl.when(swapped)
    def _():
        for q in range(8):
            pl.semaphore_signal(
                barrier, inc=1, device_id=(row(zl, y), zh * 8 + q), device_id_type=MESH
            )

    seen = present[...].astype(F32)
    own[0] = (dosage[...].astype(F32) * seen).astype(BF16)
    own[1] = seen.astype(BF16)
    design[0:COMPS, :] = comps[...]
    sub = lax.broadcasted_iota(jnp.int32, (8, people), 0)
    design[COMPS:WIDTH, :] = jnp.where(sub == 0, 1.0, 0.0).astype(F32)

    pl.semaphore_wait(barrier, jnp.where(swapped, 31, 23))

    sent = []
    names = {}

    def copy(src, dst, name, dev):
        idx = names.setdefault(name, len(names))
        return pltpu.make_async_remote_copy(
            src_ref=src, dst_ref=dst, send_sem=ssem.at[idx], recv_sem=rsem.at[idx],
            device_id=dev, device_id_type=MESH,
        )

    def push(src, dst, name, dev):
        one = copy(src, dst, name, dev)
        one.start()
        sent.append(one.wait_send)

    def pass_on(ref, name, dev):
        push(ref, ref, name, dev)

    core_dev = (r, col(zl, x, ko))

    def arrive(ref, name):
        copy(ref, ref, name, core_dev).wait_recv()

    def push_or_keep(here, src, dst, name, dev):
        one = copy(src, dst, name, dev)
        local = pltpu.make_async_copy(src, dst, lsem.at[names[name]])

        @pl.when(here)
        def _():
            local.start()

        @pl.when(jnp.logical_not(here))
        def _():
            one.start()

        def finish():
            @pl.when(jnp.logical_not(here))
            def _():
                one.wait_send()

        sent.append(finish)

    def arrive_or_keep(here, ref, name):
        one = copy(ref, ref, name, core_dev)
        local = pltpu.make_async_copy(ref, ref, lsem.at[names[name]])

        @pl.when(here)
        def _():
            local.wait()

        @pl.when(jnp.logical_not(here))
        def _():
            one.wait_recv()

    xr_dev, xl_dev = (r, col(zl, xr, k)), (r, col(zl, xl, k))
    zl_dev = (r, col(zlo, x, k))
    yr_dev, yl_dev = (row(zh, yr), c), (row(zh, yl), c)
    crosses = [zl == 1, zl == 0]
    z_dev = [(row(jnp.where(crosses[p], zho, zh), y), col(zlo, x, k)) for p in range(2)]
    zh_from = [jnp.where(crosses[1 - p], zho, zh) for p in range(2)]

    def a_slot(zl_, x_, k_, p=None):
        ref = a_out.at[col(zl_, x_, k_)]
        return ref if p is None else ref.at[p]

    def piece(ref, at):
        return ref.at[pl.ds(pl.multiple_of(8 * at, 8), 8)]

    def people_half(ref, q):
        return ref.at[:, pl.ds(pl.multiple_of(q * half, 128), half)]

    def leg1(p, q):
        push_or_keep(turn[p][q] == y, people_half(own.at[p], q), relay.at[p, q],
                     f"leg1_{p}{q}", (row(zh, turn[p][q]), c))

    leg1(0, 0)
    leg1(0, 1)
    push(own.at[0], a_slot(zl, x, k, 0), "own_xr0", xr_dev)
    push(own.at[0], a_slot(zl, x, k, 0), "own_xl0", xl_dev)
    push(own.at[0], a_slot(zl, x, k, 0), "own_zl0", zl_dev)
    leg1(1, 0)
    leg1(1, 1)
    push_or_keep(turn_mine[0] == y, people_half(piece(comps, turn_mine[0]), k), relay_c,
                 "leg1_c", (row(zh, turn_mine[0]), c))
    push(own.at[1], a_slot(zl, x, k, 1), "own_zl1", zl_dev)
    push(own, a_slot(zl, x, k), "own_core", core_dev)
    keep = pltpu.make_async_copy(own, a_out.at[c], lsem.at[127])
    keep.start()

    gram_sums(design, own, outer, acc)
    for q in range(4):
        send[q, :, 0:GRAM_ROWS] = acc[32 + 8 * q:40 + 8 * q, :]
        send[q, :, GRAM_ROWS:SUMS] = 0.5 * acc[8 * q:8 * q + 8, OFF[COMPS]:OFF[COMPS] + 128]
    wide[...] = jnp.zeros_like(wide)
    for d in range(1, 8):
        to = (r + d) % 8
        push(send.at[to % 4], recv.at[d], ("rs", d), (to, c))

    def home(p):
        return jnp.logical_and(zh == zl, turn_mine[p] == x)

    def leg2(p):
        chip_row = row(zl, y)
        for q in range(2):
            arrive_or_keep(turn[p][q] == y, relay.at[p, q], f"leg1_{p}{q}")
        push_or_keep(home(p), relay.at[p, k], b_out.at[p, c],
                     f"leg2_{p}_same", (chip_row, col(zh, turn_mine[p], k)))
        push(relay.at[p, ko], b_out.at[p, c],
             f"leg2_{p}_other", (chip_row, col(zh, turn_other[p], ko)))

    def leg2_c():
        arrive_or_keep(turn_mine[0] == y, relay_c, "leg1_c")
        push_or_keep(home(0), relay_c, piece(cb_out, y),
                     "leg2_c_same", (row(zl, y), col(zh, turn_mine[0], k)))

    def b_one(p, zh_, y_, k_):
        return b_out.at[p, 2 * row(zh_, (x + y_ + 8 - 2 * p - k) % 4) + k_]

    leg2(0)
    leg2(1)
    push(own.at[1], a_slot(zl, x, k, 1), "own_xr1", xr_dev)
    push(own.at[1], a_slot(zl, x, k, 1), "own_xl1", xl_dev)
    leg2_c()

    for p in range(2):
        arrive(a_slot(zlo, x, k, p), f"own_zl{p}")
        pass_on(a_slot(zlo, x, k, p), f"zl_xr{p}", xr_dev)
        pass_on(a_slot(zlo, x, k, p), f"zl_xl{p}", xl_dev)
    pass_on(a_slot(zlo, x, k), "zl_core", core_dev)

    core_of = [k, ko]

    def start_column(p, e):
        ref = b_one(p, zh, y, core_of[e])
        if e == 0:
            arrive_or_keep(home(p), ref, f"leg2_{p}_same")
        else:
            arrive(ref, f"leg2_{p}_other")
        push(ref, relay_z.at[p, e], f"b_mid{p}{e}", z_dev[p])
        pass_on(ref, f"b_yr{p}{e}", yr_dev)
        pass_on(ref, f"b_yl{p}{e}", yl_dev)

    def relay_column(p, e):
        arrive(relay_z.at[p, e], f"b_mid{p}{e}")
        push(relay_z.at[p, e], b_one(p, zh_from[p], y, core_of[e]), f"b_zh{p}{e}", z_dev[p])

    def turn_column(p, e):
        ref = b_one(p, zho, y, core_of[e])
        arrive(ref, f"b_zh{p}{e}")
        pass_on(ref, f"bz_yr{p}{e}", yr_dev)
        pass_on(ref, f"bz_yl{p}{e}", yl_dev)

    def far_column(p, e, zh_, tag):
        right, left = b_one(p, zh_, yl, core_of[e]), b_one(p, zh_, yr, core_of[e])
        arrive(right, f"{tag}_yr{p}{e}")
        arrive(left, f"{tag}_yl{p}{e}")
        if e == 0:
            pass_on(right, f"{tag}_far{p}{e}", yr_dev)
        else:
            pass_on(left, f"{tag}_far{p}{e}", yl_dev)

    parts = [(p, e) for p in range(2) for e in range(2)]
    for p, e in parts:
        start_column(p, e)
    total = send[r % 4]
    for d in range(1, 8):
        arrive(recv.at[d], ("rs", d))
        total = total + recv[d]
    wide[0:8, :] = total
    for q in range(SUMS // 128):
        block = wide[:, 128 * q:128 * q + 128].T
        if q < GRAM_ROWS // 128:
            gt[128 * q:128 * q + 128, :] = block
        else:
            bt[...] = block[0:WIDTH]
    solve(gt, bt, inv_s, y_s, xs)
    coef[...] = xs[...].T[0:8]
    keep_coef = pltpu.make_async_copy(coef, coef_out.at[c, y], lsem.at[126])
    keep_coef.start()
    for d in range(1, 4):
        push(coef, coef_out.at[c, y], ("cag", d), (row(zh, (y + d) % 4), c))

    for p, e in parts:
        relay_column(p, e)
    arrive_or_keep(home(0), piece(cb_out, y), "leg2_c_same")
    pass_on(piece(cb_out, y), "c_yr", yr_dev)
    pass_on(piece(cb_out, y), "c_yl", yl_dev)

    for p in range(2):
        arrive(a_slot(zl, xl, k, p), f"own_xr{p}")
        arrive(a_slot(zl, xr, k, p), f"own_xl{p}")
        if p == 0:
            pass_on(a_slot(zl, xl, k, 0), "far_xr", xr_dev)
        else:
            pass_on(a_slot(zl, xr, k, 1), "far_xl", xl_dev)
    pass_on(a_slot(zl, xl, k), "xl_core", core_dev)
    pass_on(a_slot(zl, xr, k), "xr_core", core_dev)

    for p, e in parts:
        far_column(p, e, zh, "b")
    for p, e in parts:
        turn_column(p, e)
    arrive(piece(cb_out, yl), "c_yr")
    pass_on(piece(cb_out, yl), "c_far", yr_dev)
    arrive(piece(cb_out, yr), "c_yl")

    for d in range(1, 4):
        arrive(coef_out.at[c, (y + 4 - d) % 4], ("cag", d))
    keep_coef.wait()
    for d in range(1, 16):
        push(coef_out.at[c], coef_out.at[c], ("rag", d), (r, (c + d) % 16))

    for p in range(2):
        arrive(a_slot(zlo, xl, k, p), f"zl_xr{p}")
        arrive(a_slot(zlo, xr, k, p), f"zl_xl{p}")
        if p == 0:
            pass_on(a_slot(zlo, xl, k, 0), "zfar_xr", xr_dev)
        else:
            pass_on(a_slot(zlo, xr, k, 1), "zfar_xl", xl_dev)
    pass_on(a_slot(zlo, xl, k), "zxl_core", core_dev)
    pass_on(a_slot(zlo, xr, k), "zxr_core", core_dev)
    for p, e in parts:
        far_column(p, e, zho, "bz")

    arrive(a_slot(zl, xo, k, 0), "far_xr")
    arrive(a_slot(zl, xo, k, 1), "far_xl")
    pass_on(a_slot(zl, xo, k), "far_core", core_dev)
    for p, e in parts:
        arrive(b_one(p, zh, yo, core_of[e]), f"b_far{p}{e}")
    arrive(piece(cb_out, yo), "c_far")
    arrive(a_slot(zlo, xo, k, 0), "zfar_xr")
    arrive(a_slot(zlo, xo, k, 1), "zfar_xl")
    pass_on(a_slot(zlo, xo, k), "zfar_core", core_dev)
    for p, e in parts:
        arrive(b_one(p, zho, yo, core_of[e]), f"bz_far{p}{e}")

    arrive(a_slot(zl, x, ko), "own_core")
    arrive(a_slot(zlo, x, ko), "zl_core")
    arrive(a_slot(zl, xl, ko), "xl_core")
    arrive(a_slot(zl, xr, ko), "xr_core")
    arrive(a_slot(zlo, xl, ko), "zxl_core")
    arrive(a_slot(zlo, xr, ko), "zxr_core")
    arrive(a_slot(zl, xo, ko), "far_core")
    arrive(a_slot(zlo, xo, ko), "zfar_core")
    for d in range(1, 16):
        arrive(coef_out.at[(c + 16 - d) % 16], ("rag", d))
    keep.wait()
    for finish in sent:
        finish()


def gather(dosage, present, comps):
    markers, people = dosage.shape
    half = people // 2
    any_space = pl.BlockSpec(memory_space=pl.ANY)
    vmem = pl.BlockSpec(memory_space=pltpu.VMEM)
    return pl.pallas_call(
        gather_kernel,
        out_shape=(
            jax.ShapeDtypeStruct((16, 2, markers, people), BF16),
            jax.ShapeDtypeStruct((2, 16, markers, half), BF16),
            jax.ShapeDtypeStruct((COMPS, half), F32),
            jax.ShapeDtypeStruct((16, 4, 8, 128), F32),
        ),
        in_specs=[vmem] * 3,
        out_specs=(any_space,) * 4,
        scratch_shapes=[
            pltpu.VMEM((2, markers, people), BF16),
            pltpu.VMEM((2, 2, markers, half), BF16),
            pltpu.VMEM((2, 2, markers, half), BF16),
            pltpu.VMEM((8, half), F32),
            pltpu.VMEM((WIDTH, people), F32),
            pltpu.VMEM((GRAM_ROWS, CHUNK), F32),
            pltpu.VMEM((64, GRAM_ROWS), F32),
            pltpu.VMEM((4, 8, SUMS), F32),
            pltpu.VMEM((8, 8, SUMS), F32),
            pltpu.VMEM((128, SUMS), F32),
            pltpu.VMEM((GRAM_ROWS, 128), F32),
            pltpu.VMEM((WIDTH, 128), F32),
            pltpu.VMEM((COMPS + 1, 8, 128), F32),
            pltpu.VMEM((COMPS + 1, 8, 128), F32),
            pltpu.VMEM((128, 128), F32),
            pltpu.VMEM((8, 128), F32),
            pltpu.SemaphoreType.DMA((128,)),
            pltpu.SemaphoreType.DMA((128,)),
            pltpu.SemaphoreType.DMA((128,)),
        ],
        compiler_params=pltpu.CompilerParams(collective_id=0, has_side_effects=True),
        name="gather_fit",
    )(dosage, present, comps)


def form(counts, seen, comps, coef, stack, resid, sdev):
    width = comps.shape[1]
    hi, mid, low = split3(comps)
    sub = lax.broadcasted_iota(jnp.int32, (8, width), 0)
    ones = jnp.where(sub == 0, 1.0, 0.0).astype(F32)
    zeros = jnp.zeros((8, width), F32)
    for at, part in ((0, hi), (40, hi), (80, hi), (128, mid), (168, mid), (208, low)):
        stack[at:at + COMPS, :] = part
        stack[at + COMPS:at + WIDTH, :] = ones if part is hi else zeros
    for at in (120, 248):
        stack[at:at + 8, :] = zeros
    twice = jnp.dot(coef, stack[...].astype(BF16), preferred_element_type=F32)
    twice = jnp.clip(twice, 0.02, 1.98)
    resid[...] = (counts.astype(F32) - twice).astype(BF16) * seen
    spread = twice * (2.0 - twice)
    sdev[...] = (spread * lax.rsqrt(spread)).astype(BF16) * seen


def ratio_kernel(steps, a0_ref, a1_ref, a2_ref, b_ref, c0_ref, c1_ref, c2_ref, cb_ref, coef_ref, out_ref,
                 left, rb, sb, ra0, sa0, ra1, sa1, stack, stack_b):
    tile = ra0.shape[1]
    half = rb.shape[1]
    piece = 256

    def form_a(a_ref, c_ref, ra, sa, h):
        at = slice(piece * h, piece * h + piece)
        form(a_ref[:, 0, :, at].reshape(512, piece), a_ref[:, 1, :, at].reshape(512, piece),
             c_ref[:, at], left[...], stack.at[h], ra.at[:, at], sa.at[:, at])

    @pl.when(pl.program_id(0) == 0)
    def _():
        base = coef_ref[...]
        lane = lax.broadcasted_iota(jnp.int32, base.shape, 1)
        left[:, 0:128] = base.astype(BF16)
        left[:, 128:256] = jnp.where(lane < 2 * WIDTH, base, pltpu.roll(base, 2 * WIDTH, 1)).astype(BF16)
        for h in range(half // 512):
            at = slice(512 * h, 512 * h + 512)
            form(b_ref[0, :, :, at].reshape(512, 512), b_ref[1, :, :, at].reshape(512, 512),
                 cb_ref[:, at], left[...], stack_b, rb.at[:, at], sb.at[:, at])
        for h in range(tile // piece):
            form_a(a0_ref, c0_ref, ra0, sa0, h)

    contract = (((0,), (0,)), ((), ()))

    def phase(ra, sa, row, a_ref, c_ref, rn, sn):
        for h in range(half // 256):
            at = slice(256 * h, 256 * h + 256)
            numer = lax.dot_general(ra[...], rb[:, at], contract, preferred_element_type=F32)
            denom = lax.dot_general(sa[...], sb[:, at], contract, preferred_element_type=F32)
            out_ref[row:row + tile, at] = numer / denom
            if h < tile // piece:
                form_a(a_ref, c_ref, rn, sn, h)

    phase(ra0, sa0, 0, a1_ref, c1_ref, ra1, sa1)
    phase(ra1, sa1, tile, a2_ref, c2_ref, ra0, sa0)


def ratio(a_raw, b_raw, comps, comps_b, coef):
    people = comps.shape[1]
    half = people // 2
    tile = 256
    tiles = people // tile
    whole = lambda shape: pl.BlockSpec(shape, lambda i: (0,) * len(shape), pipeline_mode=pl.Buffered(1))
    first = lambda i: 0
    odd = lambda i: 2 * i + 1
    even = lambda i: jnp.minimum(2 * i + 2, tiles - 2)
    a_spec = lambda at: pl.BlockSpec((16, 2, 32, tile), lambda i: (0, 0, 0, at(i)))
    c_spec = lambda at: pl.BlockSpec((COMPS, tile), lambda i: (0, at(i)))
    return pl.pallas_call(
        functools.partial(ratio_kernel, tiles // 2),
        out_shape=jax.ShapeDtypeStruct((people, half), F32),
        grid=(tiles // 2,),
        in_specs=[
            pl.BlockSpec((16, 2, 32, tile), lambda i: (0, 0, 0, 0), pipeline_mode=pl.Buffered(1)),
            a_spec(odd), a_spec(even),
            whole((2, 16, 32, half)),
            pl.BlockSpec((COMPS, tile), lambda i: (0, 0), pipeline_mode=pl.Buffered(1)),
            c_spec(odd), c_spec(even),
            whole((COMPS, half)),
            whole((512, 128)),
        ],
        out_specs=pl.BlockSpec((2 * tile, half), lambda i: (i, 0)),
        scratch_shapes=[
            pltpu.VMEM((512, 256), BF16),
            pltpu.VMEM((512, half), BF16),
            pltpu.VMEM((512, half), BF16),
            pltpu.VMEM((512, tile), BF16),
            pltpu.VMEM((512, tile), BF16),
            pltpu.VMEM((512, tile), BF16),
            pltpu.VMEM((512, tile), BF16),
            pltpu.VMEM((tile // 256, 256, 256), F32),
            pltpu.VMEM((256, 512), F32),
        ],
        name="form_ratio",
    )(a_raw, a_raw, a_raw, b_raw, comps, comps, comps, comps_b, coef)


def per_device(dosage, present, comps):
    a_raw, b_raw, comps_b, coef = gather(dosage, present, comps)
    return ratio(a_raw, b_raw, comps, comps_b, coef.reshape(512, 128))


def solution(mesh):
    placed = (P("cols", "rows"), P("cols", "rows"), P(None, "rows"))
    return jax.shard_map(
        per_device, mesh=mesh, in_specs=placed, out_specs=P("rows", "cols"), check_vma=False
    )
```
